32 devices in a mesh: group: 2 (over x), azim: 16 (over z, y, core).
Axes of the slice: x: 2, y: 2, z: 4, core: 2. Of those that a mesh axis runs over, the one named last changes fastest.
Arguments:
- field: bfloat16 [704, 8, 8, 640], P(('group', 'azim')), parts along dimension 0, may hold values from -6 to 6
- jacobian: bfloat16 [5, 8, 2, 320, 320], P(None, None, None, 'azim'), may hold values from -0.109375 to 0.109375
- coupling: int32 [16, 5], replicated, may hold values 0 or 1
Outputs:
- transferred: bfloat16 [704, 8, 8, 640], P(('group', 'azim')), parts along dimension 0
The draws below stay inside these ranges and needn't reach their ends.
There are 2 independent parts, one for each index of `group`. The reference program is written for one: setup_inputs(seed, part) draws one part's arguments, and reference() takes and returns one part's arrays. A program takes and returns all parts, laid end to end along the dimension named above; an argument that names none is the same for every part. Nothing has to cross between parts.
All inputs are finite; a program needn't handle non-finite values.
Results may differ from the reference program's by a relative error of at most 0.0049.
Values may be sent and summed in bfloat16 or wider, within the bound.
No kernel may reach another device: no remote copies, remote signals or barrier semaphores. Data moves between devices by JAX's collectives and lax.ppermute only.
A program may use at most 128 MiB of HBM per device.

```python
import math
import jax
import jax.numpy as jnp
from jax import lax

BLADES = 22
FREQS = 8
ORDERS = 5
AXIAL = 8
STATE = 320
PASSAGE = 16
STATIONS = 352


def touch_ends(values, key, least, high):
    shape = values.shape
    spot = [jax.random.randint(jax.random.fold_in(key, axis), (), 0, shape[axis]) for axis in range(len(shape))]
    values = values.at[tuple(spot)].set(least)
    longest = shape.index(max(shape))
    spot[longest] = (spot[longest] + 1) % shape[longest]
    return values.at[tuple(spot)].set(high)


def levels(rng, extent, cuts, least, top_value):
    def one(position, blocks):
        draws = jax.random.uniform(jax.random.fold_in(jax.random.fold_in(rng, 6), position), (blocks,), jnp.float32, least / len(cuts), top_value / len(cuts))
        return jnp.repeat(jnp.exp(draws), extent[position] // blocks).reshape((-1,) + (1,) * (len(extent) - position - 1))

    loudness = one(*cuts[0])
    for cut in cuts[1:]:
        loudness = loudness * one(*cut)
    return loudness


def noise(key, shape, scale, most, cuts=(), kind=jnp.bfloat16):
    entries = scale * jax.random.normal(key, shape, jnp.float32)
    if cuts:
        entries = entries * levels(key, shape, cuts, -0.22, 0.18)
    return jnp.clip(entries, -most, most).astype(kind)


def setup_inputs(seed: int = 0, part: int = 0) -> dict:
    splits = jax.random.split(jax.random.key(seed), 4)
    part_keys = jax.random.split(jax.random.fold_in(splits[3], part), 4)
    return {
        "field": noise(part_keys[0], (STATIONS, AXIAL, FREQS, 2 * STATE), 1.0, 6.0, ((0, 16),)),
        "jacobian": noise(splits[1], (ORDERS, FREQS, 2, STATE, STATE), (2 * STATE * ORDERS) ** -0.5, 0.109375, ((3, 16),)),
        "coupling": touch_ends((jax.random.randint(splits[2], (PASSAGE, ORDERS), 0, 4) < 3).astype(jnp.int32), jax.random.fold_in(splits[2], 1), 0, 1),
    }


def reference(field, jacobian, coupling):
    stations, axial_count, freq_count, full_width = field.shape
    half_width = full_width // 2
    item_count = axial_count * freq_count
    order_count = jacobian.shape[0]
    norm_scale = 1.0 / math.sqrt(stations)
    flattened = jnp.moveaxis(field.reshape(stations, item_count, full_width), 1, 0)
    freq_index = (jnp.arange(item_count, dtype=jnp.int32) % freq_count).astype(jnp.int32)
    gate_rows = jnp.repeat(coupling, BLADES, axis=0)

    def per_item(inputs):
        sample, freq_id = inputs
        values = sample.astype(jnp.float32)
        spectrum = jnp.fft.fft(values[:, :half_width] + 1j * values[:, half_width:], axis=0) * norm_scale
        modes = jnp.concatenate([spectrum.real, spectrum.imag], axis=1).astype(jnp.bfloat16)
        jac_item = jnp.take(jacobian, freq_id, axis=1)
        summed = jnp.zeros((stations, full_width), jnp.float32)
        for order_idx in range(order_count):
            shift_rows = (order_idx - order_count // 2) * BLADES
            moved = jnp.roll(modes, -shift_rows, axis=0) * gate_rows[:, order_idx:order_idx + 1].astype(jnp.bfloat16)
            jac_real = jac_item[order_idx, 0]
            jac_imag = jac_item[order_idx, 1]
            real_form = jnp.concatenate([jnp.concatenate([jac_real, -jac_imag], axis=1), jnp.concatenate([jac_imag, jac_real], axis=1)], axis=0)
            summed = summed + jnp.dot(moved, real_form.T, preferred_element_type=jnp.float32)
        restored = jnp.fft.ifft(summed[:, :half_width] + 1j * summed[:, half_width:], axis=0) / norm_scale
        return jnp.concatenate([restored.real, restored.imag], axis=1).astype(jnp.bfloat16)
    result = lax.map(per_item, (flattened, freq_index))
    return jnp.moveaxis(result, 0, 1).reshape(stations, axial_count, freq_count, full_width)
```

```python
import functools
import math

import jax
import jax.numpy as jnp
import ml_dtypes
import numpy as np
from jax import lax
from jax.experimental import pallas as pl
from jax.experimental.pallas import tpu as pltpu
from jax.sharding import Mesh
from jax.sharding import PartitionSpec as P

BLADES = 22
ROWS = 24


def round_up(value, multiple):
    return -(-value // multiple) * multiple


def windows(items):
    spans = []
    for item in range(items):
        first = BLADES * item
        low = first // 8 * 8
        spans.append((low, round_up(first + BLADES, 8), first - low))
    return spans


@functools.lru_cache(maxsize=None)
def phases(stations):
    index = np.arange(stations, dtype=np.int64)
    angle = (index[:, None] * index[None, :] % stations) * (2.0 * math.pi / stations)
    blocks = stations // BLADES
    shape = (blocks, BLADES, blocks, BLADES)
    return np.cos(angle).reshape(shape), np.sin(angle).reshape(shape)


def spread(block, row_span, row_at, col_span, col_at):
    count = block.shape[0]
    wide = np.zeros((count, row_span, count, col_span), np.float64)
    wide[:, row_at : row_at + BLADES, :, col_at : col_at + BLADES] = block
    return wide.reshape(count * row_span, count * col_span)


def rounded(values):
    return values.astype(np.float32).astype(ml_dtypes.bfloat16)


@functools.lru_cache(maxsize=None)
def forward_matrix(stations, span, at, split):
    pieces = []
    for part in phases(stations):
        exact = spread(part, ROWS, 0, span, at)
        head = rounded(exact)
        pieces.append(head)
        if split:
            pieces.append(rounded(exact - head.astype(np.float64)))
    return np.concatenate(pieces, axis=1)


@functools.lru_cache(maxsize=None)
def inverse_matrix(stations, span, at):
    return np.concatenate([rounded(spread(part, span, at, ROWS, 0)) for part in phases(stations)], axis=1)


def make_kernel(blocks, items, orders, width, split, spans, group):
    half = width // 2
    reach = orders // 2
    lines = round_up(ROWS * group, 16)
    norm = 1.0 / math.sqrt(blocks * BLADES)

    def body(gate_ref, data_ref, weight_ref, *rest):
        forward_refs = rest[:items]
        inverse_refs = rest[items : 2 * items]
        out_ref, modes_ref, moved_ref = rest[2 * items :]
        tail = None
        tail_at = 0
        for start in range(0, items, group):
            spectra = []
            for item in range(start, start + group):
                low, high, _ = spans[item]
                values = data_ref[:, low:high, :].reshape(blocks * (high - low), width)
                turned = jnp.concatenate([values[:, half:], -values[:, :half]], axis=1)
                stack = [values, values, turned, turned] if split else [values, turned]
                spectrum = jnp.dot(
                    forward_refs[item][...], jnp.concatenate(stack, axis=0), preferred_element_type=jnp.float32
                )
                spectra.append((spectrum * norm).reshape(blocks, ROWS, width))
            if lines > ROWS * group:
                spectra.append(jnp.zeros((blocks, lines - ROWS * group, width), jnp.float32))
            modes = jnp.concatenate(spectra, axis=1).astype(jnp.bfloat16)
            modes_ref[reach : reach + blocks] = modes
            modes_ref[:reach] = modes[blocks - reach :]
            modes_ref[reach + blocks :] = modes[:reach]
            for order in range(orders):
                for block in range(blocks):
                    piece = modes_ref[block + order]
                    keep = gate_ref[block, order] != 0
                    moved_ref[block, :, order * width : (order + 1) * width] = jnp.where(
                        keep, piece, jnp.zeros_like(piece)
                    )
            coupled = jnp.dot(
                moved_ref[...].reshape(blocks * lines, orders * width),
                weight_ref[...],
                preferred_element_type=jnp.float32,
            ).reshape(blocks, lines, width)
            for offset in range(group):
                item = start + offset
                low, high, _ = spans[item]
                own = coupled[:, offset * ROWS : (offset + 1) * ROWS].reshape(blocks * ROWS, width)
                own = own.astype(jnp.bfloat16)
                turned = jnp.concatenate([-own[:, half:], own[:, :half]], axis=1)
                result = jnp.dot(
                    inverse_refs[item][...],
                    jnp.concatenate([own, turned], axis=0),
                    preferred_element_type=jnp.float32,
                ).reshape(blocks, high - low, width)
                if tail is not None and tail_at == low:
                    joined = result[:, :8] + tail
                    result = jnp.concatenate([joined, result[:, 8:]], axis=1)
                last = item == items - 1 or spans[item + 1][0] >= high
                stop = high if last else spans[item + 1][0]
                out_ref[:, low:stop, :] = (result[:, : stop - low] * norm).astype(jnp.bfloat16)
                tail = None if last else result[:, stop - low :]
                tail_at = stop

    return body


def couple(gates, data, weights):
    blocks, lines, width = data.shape
    items = lines // BLADES
    orders = gates.shape[1]
    stations = blocks * BLADES
    spans = windows(items)
    group = 2 if items % 2 == 0 else 1
    split = True
    forward = [jnp.asarray(forward_matrix(stations, high - low, at, split)) for low, high, at in spans]
    inverse = [jnp.asarray(inverse_matrix(stations, high - low, at)) for low, high, at in spans]
    rows = round_up(ROWS * group, 16)
    in_vmem = pl.BlockSpec(memory_space=pltpu.VMEM)
    return pl.pallas_call(
        make_kernel(blocks, items, orders, width, split, spans, group),
        out_shape=jax.ShapeDtypeStruct(data.shape, jnp.bfloat16),
        in_specs=[pl.BlockSpec(memory_space=pltpu.SMEM)] + [in_vmem] * (2 + 2 * items),
        out_specs=in_vmem,
        scratch_shapes=[
            pltpu.VMEM((blocks + orders - 1, rows, width), jnp.bfloat16),
            pltpu.VMEM((blocks, rows, orders * width), jnp.bfloat16),
        ],
        compiler_params=pltpu.CompilerParams(vmem_limit_bytes=60 * 1024 * 1024),
        name="couple",
    )(gates, data, weights, *forward, *inverse)


def couple_plain(gates, data, weights):
    blocks, lines, width = data.shape
    half = width // 2
    orders = gates.shape[1]
    stations = blocks * BLADES
    norm = 1.0 / math.sqrt(stations)
    results = []
    for low, high, at in windows(lines // BLADES):
        values = data[:, low:high].reshape(blocks * (high - low), width)
        turned = jnp.concatenate([values[:, half:], -values[:, :half]], axis=1)
        spectrum = jnp.dot(
            jnp.asarray(forward_matrix(stations, high - low, at, True)),
            jnp.concatenate([values, values, turned, turned], axis=0),
            preferred_element_type=jnp.float32,
        )
        modes = (spectrum * norm).astype(jnp.bfloat16).reshape(blocks, ROWS, width)
        moved = [
            jnp.roll(modes, orders // 2 - order, axis=0) * gates[:, order].astype(jnp.bfloat16)[:, None, None]
            for order in range(orders)
        ]
        coupled = jnp.dot(
            jnp.concatenate(moved, axis=-1).reshape(blocks * ROWS, orders * width),
            weights,
            preferred_element_type=jnp.float32,
        ).astype(jnp.bfloat16)
        turned = jnp.concatenate([-coupled[:, half:], coupled[:, :half]], axis=1)
        result = jnp.dot(
            jnp.asarray(inverse_matrix(stations, high - low, at)),
            jnp.concatenate([coupled, turned], axis=0),
            preferred_element_type=jnp.float32,
        )
        own = (result * norm).astype(jnp.bfloat16).reshape(blocks, high - low, width)
        results.append(own[:, at : at + BLADES])
    joined = jnp.concatenate(results, axis=1)
    return jnp.pad(joined, ((0, 0), (0, lines - joined.shape[1]), (0, 0)))


def swap(values, axis):
    return lax.ppermute(values, axis, [(0, 1), (1, 0)])


def in_order(first, other, axis):
    mine_first = lax.axis_index(axis) == 0
    return jnp.stack([jnp.where(mine_first, first, other), jnp.where(mine_first, other, first)])


def shards(field, jacobian, coupling):
    local_stations, axial_count, freq_count, width = field.shape
    orders, _, _, own_rows, half = jacobian.shape
    peers = ("freq", "rest")
    rest = lax.axis_size("rest")
    groups = lax.axis_size("group")
    nodes = freq_count * rest
    items = axial_count // rest
    parts = groups * rest

    rows = jnp.concatenate([jacobian[:, :, 0], jacobian[:, :, 1]], axis=-1)
    if groups == 2 and rest == 2 and own_rows % parts == 0:
        piece = own_rows // parts
        rows = rows.reshape(orders, freq_count, groups, rest, piece, width).transpose(2, 1, 3, 0, 4, 5)
        mine = lax.dynamic_index_in_dim(rows, lax.axis_index("group"), 0, keepdims=False)
        mine = mine.reshape(nodes, orders * piece, width)
        got = lax.all_to_all(mine, peers, 0, 0, tiled=True)
    else:
        piece = None
        rows = rows.transpose(1, 0, 2, 3).reshape(freq_count, 1, orders * own_rows, width)
        rows = jnp.broadcast_to(rows, (freq_count, rest, orders * own_rows, width))
        got = lax.all_to_all(rows.reshape(nodes, orders * own_rows, width), peers, 0, 0, tiled=True)

    packed = field.reshape(local_stations, rest, items, freq_count, width).transpose(3, 1, 2, 0, 4)
    packed = packed.reshape(nodes, items * local_stations, width)
    lines = round_up(items * local_stations, 8)
    if lines != packed.shape[1]:
        packed = jnp.pad(packed, ((0, 0), (0, lines - packed.shape[1]), (0, 0)))
    got, packed = lax.optimization_barrier((got, packed))
    data = lax.all_to_all(packed, peers, 0, 0, tiled=True)

    if piece is not None:
        both = in_order(got, swap(got, "group"), "group")
        full = in_order(both, swap(both, "rest"), "rest")
        full = full.reshape(rest, groups, nodes, orders, piece, width).transpose(3, 2, 1, 0, 4, 5)
    else:
        full = got.reshape(nodes, orders, own_rows, width).transpose(1, 0, 2, 3)
    full = full.reshape(orders, nodes * own_rows, width)
    by_input = full.transpose(0, 2, 1)
    to_real = jnp.concatenate([by_input[:, :half], -by_input[:, half:]], axis=1)
    to_imag = jnp.concatenate([by_input[:, half:], by_input[:, :half]], axis=1)
    weights = jnp.concatenate([to_real, to_imag], axis=-1).reshape(orders * width, width)

    fits = nodes * local_stations <= 704
    result = (couple if fits else couple_plain)(coupling, data, weights)
    returned = lax.all_to_all(result, peers, 0, 0, tiled=True)[:, : items * local_stations]
    returned = returned.reshape(freq_count, rest, items, local_stations, width).transpose(3, 1, 2, 0, 4)
    return returned.reshape(local_stations, axial_count, freq_count, width)


def solution(mesh):
    names = tuple(mesh.axis_names)
    sizes = dict(mesh.shape)

    def whole(field, jacobian, coupling):
        freq_count = field.shape[2]
        devices = mesh.devices.reshape(sizes[names[0]], freq_count, sizes[names[1]] // freq_count)
        finer = Mesh(devices, ("group", "freq", "rest"))
        every = P(("group", "freq", "rest"), None, None, None)
        placed = (every, P(None, None, None, ("freq", "rest"), None), P())
        return jax.shard_map(shards, mesh=finer, in_specs=placed, out_specs=every, check_vma=False)(
            field, jacobian, coupling
        )

    return whole
```

```python
import functools
import math

import jax
import jax.numpy as jnp
import ml_dtypes
import numpy as np
from jax import lax
from jax.experimental import pallas as pl
from jax.experimental.pallas import tpu as pltpu
from jax.sharding import Mesh
from jax.sharding import PartitionSpec as P

BLADES = 22
ROWS = 24


def round_up(value, multiple):
    return -(-value // multiple) * multiple


def windows(items):
    spans = []
    for item in range(items):
        first = BLADES * item
        low = first // 8 * 8
        spans.append((low, round_up(first + BLADES, 8), first - low))
    return spans


@functools.lru_cache(maxsize=None)
def phases(stations):
    index = np.arange(stations, dtype=np.int64)
    angle = (index[:, None] * index[None, :] % stations) * (2.0 * math.pi / stations)
    blocks = stations // BLADES
    shape = (blocks, BLADES, blocks, BLADES)
    return np.cos(angle).reshape(shape), np.sin(angle).reshape(shape)


def spread(block, row_span, row_at, col_span, col_at):
    count = block.shape[0]
    wide = np.zeros((count, row_span, count, col_span), np.float64)
    wide[:, row_at : row_at + BLADES, :, col_at : col_at + BLADES] = block
    return wide.reshape(count * row_span, count * col_span)


def rounded(values):
    return values.astype(np.float32).astype(ml_dtypes.bfloat16)


@functools.lru_cache(maxsize=None)
def forward_matrix(stations, span, at, split):
    pieces = []
    for part in phases(stations):
        exact = spread(part, ROWS, 0, span, at)
        head = rounded(exact)
        pieces.append(head)
        if split:
            pieces.append(rounded(exact - head.astype(np.float64)))
    return np.concatenate(pieces, axis=1)


@functools.lru_cache(maxsize=None)
def inverse_matrix(stations, span, at):
    return np.concatenate([rounded(spread(part, span, at, ROWS, 0)) for part in phases(stations)], axis=1)


def make_kernel(blocks, items, orders, width, split, spans, group):
    half = width // 2
    reach = orders // 2
    lines = round_up(ROWS * group, 16)
    norm = 1.0 / math.sqrt(blocks * BLADES)

    def body(gate_ref, *rest):
        count = 2 + 2 * items
        far, out_ref, near = rest[:count], rest[count], rest[count + 1 : 2 * count + 1]
        modes_ref, moved_ref, sems = rest[2 * count + 1 :]
        data_ref, weight_ref = near[0], near[1]
        forward_refs, inverse_refs = near[2 : 2 + items], near[2 + items :]
        copies = [pltpu.make_async_copy(far[index], near[index], sems.at[index]) for index in range(count)]
        order_of_use = [0]
        for start in range(0, items, group):
            order_of_use += [2 + item for item in range(start, start + group)]
            order_of_use += [1] if start == 0 else []
            order_of_use += [2 + items + item for item in range(start, start + group)]
        for index in order_of_use:
            copies[index].start()
        copies[0].wait()
        tail = None
        tail_at = 0
        for start in range(0, items, group):
            spectra = []
            for item in range(start, start + group):
                low, high, _ = spans[item]
                copies[2 + item].wait()
                values = data_ref[:, low:high, :].reshape(blocks * (high - low), width)
                turned = jnp.concatenate([values[:, half:], -values[:, :half]], axis=1)
                stack = [values, values, turned, turned] if split else [values, turned]
                spectrum = jnp.dot(
                    forward_refs[item][...], jnp.concatenate(stack, axis=0), preferred_element_type=jnp.float32
                )
                spectra.append((spectrum * norm).reshape(blocks, ROWS, width))
            if lines > ROWS * group:
                spectra.append(jnp.zeros((blocks, lines - ROWS * group, width), jnp.float32))
            modes = jnp.concatenate(spectra, axis=1).astype(jnp.bfloat16)
            modes_ref[reach : reach + blocks] = modes
            modes_ref[:reach] = modes[blocks - reach :]
            modes_ref[reach + blocks :] = modes[:reach]
            for order in range(orders):
                for block in range(blocks):
                    piece = modes_ref[block + order]
                    keep = gate_ref[block, order] != 0
                    moved_ref[block, :, order * width : (order + 1) * width] = jnp.where(
                        keep, piece, jnp.zeros_like(piece)
                    )
            if start == 0:
                copies[1].wait()
            coupled = jnp.dot(
                moved_ref[...].reshape(blocks * lines, orders * width),
                weight_ref[...],
                preferred_element_type=jnp.float32,
            ).reshape(blocks, lines, width)
            for offset in range(group):
                item = start + offset
                low, high, _ = spans[item]
                own = coupled[:, offset * ROWS : (offset + 1) * ROWS].reshape(blocks * ROWS, width)
                own = own.astype(jnp.bfloat16)
                copies[2 + items + item].wait()
                turned = jnp.concatenate([-own[:, half:], own[:, :half]], axis=1)
                result = jnp.dot(
                    inverse_refs[item][...],
                    jnp.concatenate([own, turned], axis=0),
                    preferred_element_type=jnp.float32,
                ).reshape(blocks, high - low, width)
                if tail is not None and tail_at == low:
                    joined = result[:, :8] + tail
                    result = jnp.concatenate([joined, result[:, 8:]], axis=1)
                last = item == items - 1 or spans[item + 1][0] >= high
                stop = high if last else spans[item + 1][0]
                out_ref[:, low:stop, :] = (result[:, : stop - low] * norm).astype(jnp.bfloat16)
                tail = None if last else result[:, stop - low :]
                tail_at = stop

    return body


def couple(gates, data, weights):
    blocks, lines, width = data.shape
    items = lines // BLADES
    orders = gates.shape[1]
    stations = blocks * BLADES
    spans = windows(items)
    group = 2 if items % 2 == 0 else 1
    split = True
    forward = [jnp.asarray(forward_matrix(stations, high - low, at, split)) for low, high, at in spans]
    inverse = [jnp.asarray(inverse_matrix(stations, high - low, at)) for low, high, at in spans]
    rows = round_up(ROWS * group, 16)
    operands = [data, weights, *forward, *inverse]
    return pl.pallas_call(
        make_kernel(blocks, items, orders, width, split, spans, group),
        out_shape=jax.ShapeDtypeStruct(data.shape, jnp.bfloat16),
        in_specs=[pl.BlockSpec(memory_space=pltpu.SMEM)] + [pl.BlockSpec(memory_space=pltpu.HBM)] * len(operands),
        out_specs=pl.BlockSpec(memory_space=pltpu.VMEM),
        scratch_shapes=[pltpu.VMEM(operand.shape, operand.dtype) for operand in operands]
        + [
            pltpu.VMEM((blocks + orders - 1, rows, width), jnp.bfloat16),
            pltpu.VMEM((blocks, rows, orders * width), jnp.bfloat16),
            pltpu.SemaphoreType.DMA((len(operands),)),
        ],
        compiler_params=pltpu.CompilerParams(vmem_limit_bytes=60 * 1024 * 1024),
        name="couple",
    )(gates, *operands)


@functools.lru_cache(maxsize=None)
def reorder_matrix(stations, items, freqs):
    rows = np.arange(stations * items * freqs).reshape(stations, items, freqs).transpose(2, 1, 0).reshape(-1)
    return (rows[:, None] == np.arange(rows.size)[None, :]).astype(ml_dtypes.bfloat16)


def reorder_body(matrix_ref, in_ref, out_ref):
    width = in_ref.shape[-1]
    moved = jnp.dot(matrix_ref[...], in_ref[...].reshape(-1, width), preferred_element_type=jnp.float32)
    out_ref[...] = moved.astype(jnp.bfloat16).reshape(out_ref.shape)


def pack(field, rest):
    stations, axials, freqs, width = field.shape
    items = axials // rest
    matrix = jnp.asarray(reorder_matrix(stations, items, freqs))
    return pl.pallas_call(
        reorder_body,
        grid=(rest,),
        out_shape=jax.ShapeDtypeStruct((freqs, rest, items * stations, width), jnp.bfloat16),
        in_specs=[
            pl.BlockSpec(matrix.shape, lambda part: (0, 0)),
            pl.BlockSpec((stations, items, freqs, width), lambda part: (0, part, 0, 0)),
        ],
        out_specs=pl.BlockSpec((freqs, 1, items * stations, width), lambda part: (0, part, 0, 0)),
        compiler_params=pltpu.CompilerParams(vmem_limit_bytes=32 * 1024 * 1024),
        name="pack",
    )(matrix, field)


def unpack(values, axials):
    freqs, rest, lines, width = values.shape
    items = axials // rest
    stations = lines // items
    matrix = jnp.asarray(reorder_matrix(stations, items, freqs).T)
    return pl.pallas_call(
        reorder_body,
        grid=(rest,),
        out_shape=jax.ShapeDtypeStruct((stations, axials, freqs, width), jnp.bfloat16),
        in_specs=[
            pl.BlockSpec(matrix.shape, lambda part: (0, 0)),
            pl.BlockSpec((freqs, 1, lines, width), lambda part: (0, part, 0, 0)),
        ],
        out_specs=pl.BlockSpec((stations, items, freqs, width), lambda part: (0, part, 0, 0)),
        compiler_params=pltpu.CompilerParams(vmem_limit_bytes=32 * 1024 * 1024),
        name="unpack",
    )(matrix, values)


def real_form_body(in_ref, out_ref):
    width = in_ref.shape[-1]
    half = width // 2
    by_input = in_ref[0].astype(jnp.float32).T
    real, imag = by_input[:half], by_input[half:]
    out_ref[:half] = jnp.concatenate([real, imag], axis=1).astype(jnp.bfloat16)
    out_ref[half:] = jnp.concatenate([-imag, real], axis=1).astype(jnp.bfloat16)


def real_form(full):
    orders, half, width = full.shape
    return pl.pallas_call(
        real_form_body,
        grid=(orders,),
        out_shape=jax.ShapeDtypeStruct((orders * width, width), jnp.bfloat16),
        in_specs=[pl.BlockSpec((1, half, width), lambda order: (order, 0, 0))],
        out_specs=pl.BlockSpec((width, width), lambda order: (order, 0)),
        compiler_params=pltpu.CompilerParams(vmem_limit_bytes=24 * 1024 * 1024),
        name="real_form",
    )(full)


def couple_plain(gates, data, weights):
    blocks, lines, width = data.shape
    half = width // 2
    orders = gates.shape[1]
    stations = blocks * BLADES
    norm = 1.0 / math.sqrt(stations)
    results = []
    for low, high, at in windows(lines // BLADES):
        values = data[:, low:high].reshape(blocks * (high - low), width)
        turned = jnp.concatenate([values[:, half:], -values[:, :half]], axis=1)
        spectrum = jnp.dot(
            jnp.asarray(forward_matrix(stations, high - low, at, True)),
            jnp.concatenate([values, values, turned, turned], axis=0),
            preferred_element_type=jnp.float32,
        )
        modes = (spectrum * norm).astype(jnp.bfloat16).reshape(blocks, ROWS, width)
        moved = [
            jnp.roll(modes, orders // 2 - order, axis=0) * gates[:, order].astype(jnp.bfloat16)[:, None, None]
            for order in range(orders)
        ]
        coupled = jnp.dot(
            jnp.concatenate(moved, axis=-1).reshape(blocks * ROWS, orders * width),
            weights,
            preferred_element_type=jnp.float32,
        ).astype(jnp.bfloat16)
        turned = jnp.concatenate([-coupled[:, half:], coupled[:, :half]], axis=1)
        result = jnp.dot(
            jnp.asarray(inverse_matrix(stations, high - low, at)),
            jnp.concatenate([coupled, turned], axis=0),
            preferred_element_type=jnp.float32,
        )
        own = (result * norm).astype(jnp.bfloat16).reshape(blocks, high - low, width)
        results.append(own[:, at : at + BLADES])
    joined = jnp.concatenate(results, axis=1)
    return jnp.pad(joined, ((0, 0), (0, lines - joined.shape[1]), (0, 0)))


def swap(values, axis):
    return lax.ppermute(values, axis, [(0, 1), (1, 0)])


def in_order(first, other, axis):
    mine_first = lax.axis_index(axis) == 0
    return jnp.stack([jnp.where(mine_first, first, other), jnp.where(mine_first, other, first)])


def shards(field, jacobian, coupling):
    local_stations, axial_count, freq_count, width = field.shape
    orders, _, _, own_rows, half = jacobian.shape
    peers = ("freq", "rest")
    rest = lax.axis_size("rest")
    groups = lax.axis_size("group")
    nodes = freq_count * rest
    items = axial_count // rest
    parts = groups * rest

    shared = groups == 2 and rest == 2 and own_rows % 2 == 0
    if shared:
        piece = own_rows // 2
        rows = jacobian.reshape(orders, freq_count, 2, 2, piece, half).transpose(3, 1, 0, 4, 2, 5)
        mine = lax.dynamic_index_in_dim(rows, lax.axis_index("group"), 0, keepdims=False)
        chip = lax.axis_index("freq")
        got = []
        for step in range(freq_count):
            block = lax.dynamic_index_in_dim(mine, chip ^ step, 0, keepdims=False)
            pairs = [(index, index ^ step) for index in range(freq_count)]
            got.append(lax.ppermute(block, "freq", pairs) if step else block)
    else:
        rows = jnp.concatenate([jacobian[:, :, 0], jacobian[:, :, 1]], axis=-1)
        rows = rows.transpose(1, 0, 2, 3).reshape(freq_count, 1, orders * own_rows, width)
        rows = jnp.broadcast_to(rows, (freq_count, rest, orders * own_rows, width))
        got = lax.all_to_all(rows.reshape(nodes, orders * own_rows, width), peers, 0, 0, tiled=True)

    fits = nodes * local_stations <= 704 and items * local_stations % 8 == 0
    if fits:
        packed = pack(field, rest).reshape(nodes, items * local_stations, width)
    else:
        packed = field.reshape(local_stations, rest, items, freq_count, width).transpose(3, 1, 2, 0, 4)
        packed = packed.reshape(nodes, items * local_stations, width)
    lines = round_up(items * local_stations, 8)
    if lines != packed.shape[1]:
        packed = jnp.pad(packed, ((0, 0), (0, lines - packed.shape[1]), (0, 0)))
    got, packed = lax.optimization_barrier((got, packed))
    data = lax.all_to_all(packed, peers, 0, 0, tiled=True)

    if shared:
        ordered = jnp.stack(got)
        for bit in range(freq_count.bit_length() - 1):
            halves = ordered.reshape((freq_count >> (bit + 1), 2, 1 << bit) + ordered.shape[1:])
            flipped = jnp.where((chip >> bit) & 1 == 1, halves[:, ::-1], halves)
            ordered = flipped.reshape(ordered.shape)
        both = in_order(ordered, swap(ordered, "group"), "group")
        full = in_order(both, swap(both, "rest"), "rest")
        full = full.transpose(3, 2, 0, 1, 4, 5, 6)
    else:
        full = got.reshape(nodes, orders, own_rows, width).transpose(1, 0, 2, 3)
    full = full.reshape(orders, nodes * own_rows, width)
    weights = real_form(full)

    result = (couple if fits else couple_plain)(coupling, data, weights)
    returned = lax.all_to_all(result, peers, 0, 0, tiled=True)
    if fits:
        return unpack(returned.reshape(freq_count, rest, items * local_stations, width), axial_count)
    returned = returned[:, : items * local_stations]
    returned = returned.reshape(freq_count, rest, items, local_stations, width).transpose(3, 1, 2, 0, 4)
    return returned.reshape(local_stations, axial_count, freq_count, width)


def solution(mesh):
    names = tuple(mesh.axis_names)
    sizes = dict(mesh.shape)

    def whole(field, jacobian, coupling):
        freq_count = field.shape[2]
        devices = mesh.devices.reshape(sizes[names[0]], freq_count, sizes[names[1]] // freq_count)
        finer = Mesh(devices, ("group", "freq", "rest"))
        every = P(("group", "freq", "rest"), None, None, None)
        placed = (every, P(None, None, None, ("freq", "rest"), None), P())
        return jax.shard_map(shards, mesh=finer, in_specs=placed, out_specs=every, check_vma=False)(
            field, jacobian, coupling
        )

    return whole
```

```python
import functools
import math

import jax
import jax.numpy as jnp
import ml_dtypes
import numpy as np
from jax import lax
from jax.experimental import pallas as pl
from jax.experimental.pallas import tpu as pltpu
from jax.sharding import Mesh
from jax.sharding import PartitionSpec as P

BLADES = 22
ROWS = 24


def round_up(value, multiple):
    return -(-value // multiple) * multiple


def windows(items):
    spans = []
    for item in range(items):
        first = BLADES * item
        low = first // 8 * 8
        spans.append((low, round_up(first + BLADES, 8), first - low))
    return spans


@functools.lru_cache(maxsize=None)
def phases(stations):
    index = np.arange(stations, dtype=np.int64)
    angle = (index[:, None] * index[None, :] % stations) * (2.0 * math.pi / stations)
    blocks = stations // BLADES
    shape = (blocks, BLADES, blocks, BLADES)
    return np.cos(angle).reshape(shape), np.sin(angle).reshape(shape)


def spread(block, row_span, row_at, col_span, col_at):
    count = block.shape[0]
    wide = np.zeros((count, row_span, count, col_span), np.float64)
    wide[:, row_at : row_at + BLADES, :, col_at : col_at + BLADES] = block
    return wide.reshape(count * row_span, count * col_span)


def rounded(values):
    return values.astype(np.float32).astype(ml_dtypes.bfloat16)


@functools.lru_cache(maxsize=None)
def forward_matrix(stations, span, at, split):
    pieces = []
    for part in phases(stations):
        exact = spread(part, ROWS, 0, span, at)
        head = rounded(exact)
        pieces.append(head)
        if split:
            pieces.append(rounded(exact - head.astype(np.float64)))
    return np.concatenate(pieces, axis=1)


@functools.lru_cache(maxsize=None)
def inverse_matrix(stations, span, at):
    return np.concatenate([rounded(spread(part, span, at, ROWS, 0)) for part in phases(stations)], axis=1)


def product(read, right, count, pieces):
    size = count // pieces
    parts = [
        jnp.dot(read(piece * size, size), right, preferred_element_type=jnp.float32) for piece in range(pieces)
    ]
    return jnp.concatenate(parts, axis=0)


def make_kernel(blocks, items, orders, width, split, spans, group):
    half = width // 2
    reach = orders // 2
    lines = round_up(ROWS * group, 16)
    norm = 1.0 / math.sqrt(blocks * BLADES)

    def body(gate_ref, *rest):
        count = 2 + 2 * items
        far, out_ref, near = rest[:count], rest[count], rest[count + 1 : 2 * count + 1]
        modes_ref, moved_ref, sems = rest[2 * count + 1 :]
        data_ref, weight_ref = near[0], near[1]
        forward_refs, inverse_refs = near[2 : 2 + items], near[2 + items :]
        copies = [pltpu.make_async_copy(far[index], near[index], sems.at[index]) for index in range(count)]
        order_of_use = [0]
        for start in range(0, items, group):
            order_of_use += [2 + item for item in range(start, start + group)]
            order_of_use += [1] if start == 0 else []
            order_of_use += [2 + items + item for item in range(start, start + group)]
        for index in order_of_use:
            copies[index].start()
        copies[0].wait()
        tail = None
        tail_at = 0
        for start in range(0, items, group):
            spectra = []
            for item in range(start, start + group):
                low, high, _ = spans[item]
                copies[2 + item].wait()
                values = data_ref[:, low:high, :].reshape(blocks * (high - low), width)
                turned = jnp.concatenate([values[:, half:], -values[:, :half]], axis=1)
                stack = [values, values, turned, turned] if split else [values, turned]
                forward_ref = forward_refs[item]
                spectrum = product(
                    lambda first, size, ref=forward_ref: ref[first : first + size],
                    jnp.concatenate(stack, axis=0),
                    blocks * ROWS,
                    2,
                )
                spectra.append((spectrum * norm).reshape(blocks, ROWS, width))
            if lines > ROWS * group:
                spectra.append(jnp.zeros((blocks, lines - ROWS * group, width), jnp.float32))
            modes = jnp.concatenate(spectra, axis=1).astype(jnp.bfloat16)
            modes_ref[reach : reach + blocks] = modes
            modes_ref[:reach] = modes[blocks - reach :]
            modes_ref[reach + blocks :] = modes[:reach]
            for order in range(orders):
                for block in range(blocks):
                    piece = modes_ref[block + order]
                    keep = gate_ref[block, order] != 0
                    moved_ref[block, :, order * width : (order + 1) * width] = jnp.where(
                        keep, piece, jnp.zeros_like(piece)
                    )
            if start == 0:
                copies[1].wait()
            coupled = product(
                lambda first, size: moved_ref[first : first + size].reshape(size * lines, orders * width),
                weight_ref[...],
                blocks,
                4,
            ).reshape(blocks, lines, width)
            for offset in range(group):
                item = start + offset
                low, high, _ = spans[item]
                own = coupled[:, offset * ROWS : (offset + 1) * ROWS].reshape(blocks * ROWS, width)
                own = own.astype(jnp.bfloat16)
                copies[2 + items + item].wait()
                turned = jnp.concatenate([-own[:, half:], own[:, :half]], axis=1)
                inverse_ref = inverse_refs[item]
                result = product(
                    lambda first, size, ref=inverse_ref: ref[first : first + size],
                    jnp.concatenate([own, turned], axis=0),
                    blocks * (high - low),
                    2,
                ).reshape(blocks, high - low, width)
                if tail is not None and tail_at == low:
                    joined = result[:, :8] + tail
                    result = jnp.concatenate([joined, result[:, 8:]], axis=1)
                last = item == items - 1 or spans[item + 1][0] >= high
                stop = high if last else spans[item + 1][0]
                out_ref[:, low:stop, :] = (result[:, : stop - low] * norm).astype(jnp.bfloat16)
                tail = None if last else result[:, stop - low :]
                tail_at = stop

    return body


def couple(gates, data, weights):
    blocks, lines, width = data.shape
    items = lines // BLADES
    orders = gates.shape[1]
    stations = blocks * BLADES
    spans = windows(items)
    group = 2 if items % 2 == 0 else 1
    split = True
    forward = [jnp.asarray(forward_matrix(stations, high - low, at, split)) for low, high, at in spans]
    inverse = [jnp.asarray(inverse_matrix(stations, high - low, at)) for low, high, at in spans]
    rows = round_up(ROWS * group, 16)
    operands = [data, weights, *forward, *inverse]
    return pl.pallas_call(
        make_kernel(blocks, items, orders, width, split, spans, group),
        out_shape=jax.ShapeDtypeStruct(data.shape, jnp.bfloat16),
        in_specs=[pl.BlockSpec(memory_space=pltpu.SMEM)] + [pl.BlockSpec(memory_space=pltpu.HBM)] * len(operands),
        out_specs=pl.BlockSpec(memory_space=pltpu.VMEM),
        scratch_shapes=[pltpu.VMEM(operand.shape, operand.dtype) for operand in operands]
        + [
            pltpu.VMEM((blocks + orders - 1, rows, width), jnp.bfloat16),
            pltpu.VMEM((blocks, rows, orders * width), jnp.bfloat16),
            pltpu.SemaphoreType.DMA((len(operands),)),
        ],
        compiler_params=pltpu.CompilerParams(vmem_limit_bytes=60 * 1024 * 1024),
        name="couple",
    )(gates, *operands)


@functools.lru_cache(maxsize=None)
def reorder_matrix(stations, items, freqs):
    rows = np.arange(stations * items * freqs).reshape(stations, items, freqs).transpose(2, 1, 0).reshape(-1)
    return (rows[:, None] == np.arange(rows.size)[None, :]).astype(ml_dtypes.bfloat16)


def reorder_body(matrix_ref, in_ref, out_ref):
    width = in_ref.shape[-1]
    moved = jnp.dot(matrix_ref[...], in_ref[...].reshape(-1, width), preferred_element_type=jnp.float32)
    out_ref[...] = moved.astype(jnp.bfloat16).reshape(out_ref.shape)


def pack(field, rest):
    stations, axials, freqs, width = field.shape
    items = axials // rest
    matrix = jnp.asarray(reorder_matrix(stations, items, freqs))
    return pl.pallas_call(
        reorder_body,
        grid=(rest,),
        out_shape=jax.ShapeDtypeStruct((freqs, rest, items * stations, width), jnp.bfloat16),
        in_specs=[
            pl.BlockSpec(matrix.shape, lambda part: (0, 0)),
            pl.BlockSpec((stations, items, freqs, width), lambda part: (0, part, 0, 0)),
        ],
        out_specs=pl.BlockSpec((freqs, 1, items * stations, width), lambda part: (0, part, 0, 0)),
        compiler_params=pltpu.CompilerParams(vmem_limit_bytes=32 * 1024 * 1024),
        name="pack",
    )(matrix, field)


def unpack(values, axials):
    freqs, rest, lines, width = values.shape
    items = axials // rest
    stations = lines // items
    matrix = jnp.asarray(reorder_matrix(stations, items, freqs).T)
    return pl.pallas_call(
        reorder_body,
        grid=(rest,),
        out_shape=jax.ShapeDtypeStruct((stations, axials, freqs, width), jnp.bfloat16),
        in_specs=[
            pl.BlockSpec(matrix.shape, lambda part: (0, 0)),
            pl.BlockSpec((freqs, 1, lines, width), lambda part: (0, part, 0, 0)),
        ],
        out_specs=pl.BlockSpec((stations, items, freqs, width), lambda part: (0, part, 0, 0)),
        compiler_params=pltpu.CompilerParams(vmem_limit_bytes=32 * 1024 * 1024),
        name="unpack",
    )(matrix, values)


def real_form_body(in_ref, out_ref):
    width = in_ref.shape[-1]
    half = width // 2
    by_input = in_ref[0].astype(jnp.float32).T
    real, imag = by_input[:half], by_input[half:]
    out_ref[:half] = jnp.concatenate([real, imag], axis=1).astype(jnp.bfloat16)
    out_ref[half:] = jnp.concatenate([-imag, real], axis=1).astype(jnp.bfloat16)


def real_form(full):
    orders, half, width = full.shape
    return pl.pallas_call(
        real_form_body,
        grid=(orders,),
        out_shape=jax.ShapeDtypeStruct((orders * width, width), jnp.bfloat16),
        in_specs=[pl.BlockSpec((1, half, width), lambda order: (order, 0, 0))],
        out_specs=pl.BlockSpec((width, width), lambda order: (order, 0)),
        compiler_params=pltpu.CompilerParams(vmem_limit_bytes=24 * 1024 * 1024),
        name="real_form",
    )(full)


def couple_plain(gates, data, weights):
    blocks, lines, width = data.shape
    half = width // 2
    orders = gates.shape[1]
    stations = blocks * BLADES
    norm = 1.0 / math.sqrt(stations)
    results = []
    for low, high, at in windows(lines // BLADES):
        values = data[:, low:high].reshape(blocks * (high - low), width)
        turned = jnp.concatenate([values[:, half:], -values[:, :half]], axis=1)
        spectrum = jnp.dot(
            jnp.asarray(forward_matrix(stations, high - low, at, True)),
            jnp.concatenate([values, values, turned, turned], axis=0),
            preferred_element_type=jnp.float32,
        )
        modes = (spectrum * norm).astype(jnp.bfloat16).reshape(blocks, ROWS, width)
        moved = [
            jnp.roll(modes, orders // 2 - order, axis=0) * gates[:, order].astype(jnp.bfloat16)[:, None, None]
            for order in range(orders)
        ]
        coupled = jnp.dot(
            jnp.concatenate(moved, axis=-1).reshape(blocks * ROWS, orders * width),
            weights,
            preferred_element_type=jnp.float32,
        ).astype(jnp.bfloat16)
        turned = jnp.concatenate([-coupled[:, half:], coupled[:, :half]], axis=1)
        result = jnp.dot(
            jnp.asarray(inverse_matrix(stations, high - low, at)),
            jnp.concatenate([coupled, turned], axis=0),
            preferred_element_type=jnp.float32,
        )
        own = (result * norm).astype(jnp.bfloat16).reshape(blocks, high - low, width)
        results.append(own[:, at : at + BLADES])
    joined = jnp.concatenate(results, axis=1)
    return jnp.pad(joined, ((0, 0), (0, lines - joined.shape[1]), (0, 0)))


def swap(values, axis):
    return lax.ppermute(values, axis, [(0, 1), (1, 0)])


def in_order(first, other, axis):
    mine_first = lax.axis_index(axis) == 0
    return jnp.stack([jnp.where(mine_first, first, other), jnp.where(mine_first, other, first)])


def shards(field, jacobian, coupling):
    local_stations, axial_count, freq_count, width = field.shape
    orders, _, _, own_rows, half = jacobian.shape
    peers = ("freq", "rest")
    rest = lax.axis_size("rest")
    groups = lax.axis_size("group")
    nodes = freq_count * rest
    items = axial_count // rest
    parts = groups * rest

    shared = groups == 2 and rest == 2 and own_rows % 2 == 0
    if shared:
        piece = own_rows // 2
        rows = jacobian.reshape(orders, freq_count, 2, 2, piece, half).transpose(3, 1, 0, 4, 2, 5)
        mine = lax.dynamic_index_in_dim(rows, lax.axis_index("group"), 0, keepdims=False)
        chip = lax.axis_index("freq")
        got = []
        for step in range(freq_count):
            block = lax.dynamic_index_in_dim(mine, chip ^ step, 0, keepdims=False)
            pairs = [(index, index ^ step) for index in range(freq_count)]
            got.append(lax.ppermute(block, "freq", pairs) if step else block)
    else:
        rows = jnp.concatenate([jacobian[:, :, 0], jacobian[:, :, 1]], axis=-1)
        rows = rows.transpose(1, 0, 2, 3).reshape(freq_count, 1, orders * own_rows, width)
        rows = jnp.broadcast_to(rows, (freq_count, rest, orders * own_rows, width))
        got = lax.all_to_all(rows.reshape(nodes, orders * own_rows, width), peers, 0, 0, tiled=True)

    fits = nodes * local_stations <= 704 and items * local_stations % 8 == 0
    if fits:
        packed = pack(field, rest).reshape(nodes, items * local_stations, width)
    else:
        packed = field.reshape(local_stations, rest, items, freq_count, width).transpose(3, 1, 2, 0, 4)
        packed = packed.reshape(nodes, items * local_stations, width)
    lines = round_up(items * local_stations, 8)
    if lines != packed.shape[1]:
        packed = jnp.pad(packed, ((0, 0), (0, lines - packed.shape[1]), (0, 0)))
    got, packed = lax.optimization_barrier((got, packed))
    data = lax.all_to_all(packed, peers, 0, 0, tiled=True)

    if shared:
        ordered = jnp.stack(got)
        for bit in range(freq_count.bit_length() - 1):
            halves = ordered.reshape((freq_count >> (bit + 1), 2, 1 << bit) + ordered.shape[1:])
            flipped = jnp.where((chip >> bit) & 1 == 1, halves[:, ::-1], halves)
            ordered = flipped.reshape(ordered.shape)
        both = in_order(ordered, swap(ordered, "group"), "group")
        full = in_order(both, swap(both, "rest"), "rest")
        full = full.transpose(3, 2, 0, 1, 4, 5, 6)
    else:
        full = got.reshape(nodes, orders, own_rows, width).transpose(1, 0, 2, 3)
    full = full.reshape(orders, nodes * own_rows, width)
    weights = real_form(full)

    result = (couple if fits else couple_plain)(coupling, data, weights)
    returned = lax.all_to_all(result, peers, 0, 0, tiled=True)
    if fits:
        return unpack(returned.reshape(freq_count, rest, items * local_stations, width), axial_count)
    returned = returned[:, : items * local_stations]
    returned = returned.reshape(freq_count, rest, items, local_stations, width).transpose(3, 1, 2, 0, 4)
    return returned.reshape(local_stations, axial_count, freq_count, width)


def solution(mesh):
    names = tuple(mesh.axis_names)
    sizes = dict(mesh.shape)

    def whole(field, jacobian, coupling):
        freq_count = field.shape[2]
        devices = mesh.devices.reshape(sizes[names[0]], freq_count, sizes[names[1]] // freq_count)
        finer = Mesh(devices, ("group", "freq", "rest"))
        every = P(("group", "freq", "rest"), None, None, None)
        placed = (every, P(None, None, None, ("freq", "rest"), None), P())
        return jax.shard_map(shards, mesh=finer, in_specs=placed, out_specs=every, check_vma=False)(
            field, jacobian, coupling
        )

    return whole
```

```python
import functools
import math

import jax
import jax.numpy as jnp
import ml_dtypes
import numpy as np
from jax import lax
from jax.experimental import pallas as pl
from jax.experimental.pallas import tpu as pltpu
from jax.sharding import Mesh
from jax.sharding import PartitionSpec as P

BLADES = 22
ROWS = 24


def round_up(value, multiple):
    return -(-value // multiple) * multiple


def windows(items):
    spans = []
    for item in range(items):
        first = BLADES * item
        low = first // 8 * 8
        spans.append((low, round_up(first + BLADES, 8), first - low))
    return spans


@functools.lru_cache(maxsize=None)
def phases(stations):
    index = np.arange(stations, dtype=np.int64)
    angle = (index[:, None] * index[None, :] % stations) * (2.0 * math.pi / stations)
    blocks = stations // BLADES
    shape = (blocks, BLADES, blocks, BLADES)
    return np.cos(angle).reshape(shape), np.sin(angle).reshape(shape)


def spread(block, row_span, row_at, col_span, col_at):
    count = block.shape[0]
    wide = np.zeros((count, row_span, count, col_span), np.float64)
    wide[:, row_at : row_at + BLADES, :, col_at : col_at + BLADES] = block
    return wide.reshape(count * row_span, count * col_span)


def rounded(values):
    return values.astype(np.float32).astype(ml_dtypes.bfloat16)


@functools.lru_cache(maxsize=None)
def forward_matrix(stations, span, at, split):
    pieces = []
    for part in phases(stations):
        exact = spread(part, ROWS, 0, span, at)
        head = rounded(exact)
        pieces.append(head)
        if split:
            pieces.append(rounded(exact - head.astype(np.float64)))
    return np.concatenate(pieces, axis=1)


@functools.lru_cache(maxsize=None)
def inverse_matrix(stations, span, at):
    return np.concatenate([rounded(spread(part, span, at, ROWS, 0)) for part in phases(stations)], axis=1)


def product(read, right, count, pieces):
    size = count // pieces
    parts = [
        jnp.dot(read(piece * size, size), right, preferred_element_type=jnp.float32) for piece in range(pieces)
    ]
    return jnp.concatenate(parts, axis=0)


def make_kernel(blocks, items, orders, width, split, spans, group):
    half = width // 2
    reach = orders // 2
    lines = round_up(ROWS * group, 16)
    norm = 1.0 / math.sqrt(blocks * BLADES)

    def body(gate_ref, *rest):
        count = 2 + 2 * items
        far, out_hbm, near = rest[:count], rest[count], rest[count + 1 : 2 * count + 1]
        modes_ref, moved_ref, out_ref, sems, out_sems = rest[2 * count + 1 :]
        data_ref, weight_ref = near[0], near[1]
        forward_refs, inverse_refs = near[2 : 2 + items], near[2 + items :]
        copies = [pltpu.make_async_copy(far[index], near[index], sems.at[index]) for index in range(count)]
        order_of_use = [0]
        for start in range(0, items, group):
            order_of_use += [2 + item for item in range(start, start + group)]
            order_of_use += [1] if start == 0 else []
            order_of_use += [2 + items + item for item in range(start, start + group)]
        for index in order_of_use:
            copies[index].start()
        copies[0].wait()
        leaving = []
        tail = None
        tail_at = 0
        for start in range(0, items, group):
            spectra = []
            for item in range(start, start + group):
                low, high, _ = spans[item]
                copies[2 + item].wait()
                values = data_ref[:, low:high, :].reshape(blocks * (high - low), width)
                turned = jnp.concatenate([values[:, half:], -values[:, :half]], axis=1)
                stack = [values, values, turned, turned] if split else [values, turned]
                forward_ref = forward_refs[item]
                spectrum = product(
                    lambda first, size, ref=forward_ref: ref[first : first + size],
                    jnp.concatenate(stack, axis=0),
                    blocks * ROWS,
                    2,
                )
                spectra.append((spectrum * norm).reshape(blocks, ROWS, width))
            if lines > ROWS * group:
                spectra.append(jnp.zeros((blocks, lines - ROWS * group, width), jnp.float32))
            modes = jnp.concatenate(spectra, axis=1).astype(jnp.bfloat16)
            modes_ref[reach : reach + blocks] = modes
            modes_ref[:reach] = modes[blocks - reach :]
            modes_ref[reach + blocks :] = modes[:reach]
            for order in range(orders):
                for block in range(blocks):
                    piece = modes_ref[block + order]
                    keep = gate_ref[block, order] != 0
                    moved_ref[block, :, order * width : (order + 1) * width] = jnp.where(
                        keep, piece, jnp.zeros_like(piece)
                    )
            if start == 0:
                copies[1].wait()
            coupled = product(
                lambda first, size: moved_ref[first : first + size].reshape(size * lines, orders * width),
                weight_ref[...],
                blocks,
                2,
            ).reshape(blocks, lines, width)
            for offset in range(group):
                item = start + offset
                low, high, _ = spans[item]
                own = coupled[:, offset * ROWS : (offset + 1) * ROWS].reshape(blocks * ROWS, width)
                own = own.astype(jnp.bfloat16)
                copies[2 + items + item].wait()
                turned = jnp.concatenate([-own[:, half:], own[:, :half]], axis=1)
                inverse_ref = inverse_refs[item]
                result = product(
                    lambda first, size, ref=inverse_ref: ref[first : first + size],
                    jnp.concatenate([own, turned], axis=0),
                    blocks * (high - low),
                    2,
                ).reshape(blocks, high - low, width)
                if tail is not None and tail_at == low:
                    joined = result[:, :8] + tail
                    result = jnp.concatenate([joined, result[:, 8:]], axis=1)
                last = item == items - 1 or spans[item + 1][0] >= high
                stop = high if last else spans[item + 1][0]
                out_ref[:, low:stop, :] = (result[:, : stop - low] * norm).astype(jnp.bfloat16)
                leaving.append(
                    pltpu.make_async_copy(out_ref.at[:, low:stop], out_hbm.at[:, low:stop], out_sems.at[item])
                )
                leaving[-1].start()
                tail = None if last else result[:, stop - low :]
                tail_at = stop
        for copy in leaving:
            copy.wait()

    return body


def couple(gates, data, weights):
    blocks, lines, width = data.shape
    items = lines // BLADES
    orders = gates.shape[1]
    stations = blocks * BLADES
    spans = windows(items)
    group = 2 if items % 2 == 0 else 1
    split = True
    forward = [jnp.asarray(forward_matrix(stations, high - low, at, split)) for low, high, at in spans]
    inverse = [jnp.asarray(inverse_matrix(stations, high - low, at)) for low, high, at in spans]
    rows = round_up(ROWS * group, 16)
    operands = [data, weights, *forward, *inverse]
    return pl.pallas_call(
        make_kernel(blocks, items, orders, width, split, spans, group),
        out_shape=jax.ShapeDtypeStruct(data.shape, jnp.bfloat16),
        in_specs=[pl.BlockSpec(memory_space=pltpu.SMEM)] + [pl.BlockSpec(memory_space=pltpu.HBM)] * len(operands),
        out_specs=pl.BlockSpec(memory_space=pltpu.HBM),
        scratch_shapes=[pltpu.VMEM(operand.shape, operand.dtype) for operand in operands]
        + [
            pltpu.VMEM((blocks + orders - 1, rows, width), jnp.bfloat16),
            pltpu.VMEM((blocks, rows, orders * width), jnp.bfloat16),
            pltpu.VMEM(data.shape, jnp.bfloat16),
            pltpu.SemaphoreType.DMA((len(operands),)),
            pltpu.SemaphoreType.DMA((items,)),
        ],
        compiler_params=pltpu.CompilerParams(vmem_limit_bytes=60 * 1024 * 1024),
        name="couple",
    )(gates, *operands)


@functools.lru_cache(maxsize=None)
def reorder_matrix(stations, items, freqs):
    rows = np.arange(stations * items * freqs).reshape(stations, items, freqs).transpose(2, 1, 0).reshape(-1)
    return (rows[:, None] == np.arange(rows.size)[None, :]).astype(ml_dtypes.bfloat16)


def reorder_body(matrix_ref, in_ref, out_ref):
    width = in_ref.shape[-1]
    moved = jnp.dot(matrix_ref[...], in_ref[...].reshape(-1, width), preferred_element_type=jnp.float32)
    out_ref[...] = moved.astype(jnp.bfloat16).reshape(out_ref.shape)


def pack(field, rest):
    stations, axials, freqs, width = field.shape
    items = axials // rest
    matrix = jnp.asarray(reorder_matrix(stations, items, freqs))
    return pl.pallas_call(
        reorder_body,
        grid=(rest,),
        out_shape=jax.ShapeDtypeStruct((freqs, rest, items * stations, width), jnp.bfloat16),
        in_specs=[
            pl.BlockSpec(matrix.shape, lambda part: (0, 0)),
            pl.BlockSpec((stations, items, freqs, width), lambda part: (0, part, 0, 0)),
        ],
        out_specs=pl.BlockSpec((freqs, 1, items * stations, width), lambda part: (0, part, 0, 0)),
        compiler_params=pltpu.CompilerParams(vmem_limit_bytes=32 * 1024 * 1024),
        name="pack",
    )(matrix, field)


def unpack(values, axials):
    freqs, rest, lines, width = values.shape
    items = axials // rest
    stations = lines // items
    matrix = jnp.asarray(reorder_matrix(stations, items, freqs).T)
    return pl.pallas_call(
        reorder_body,
        grid=(rest,),
        out_shape=jax.ShapeDtypeStruct((stations, axials, freqs, width), jnp.bfloat16),
        in_specs=[
            pl.BlockSpec(matrix.shape, lambda part: (0, 0)),
            pl.BlockSpec((freqs, 1, lines, width), lambda part: (0, part, 0, 0)),
        ],
        out_specs=pl.BlockSpec((stations, items, freqs, width), lambda part: (0, part, 0, 0)),
        compiler_params=pltpu.CompilerParams(vmem_limit_bytes=32 * 1024 * 1024),
        name="unpack",
    )(matrix, values)


def real_form_body(in_ref, out_ref):
    width = in_ref.shape[-1]
    half = width // 2
    by_input = in_ref[0].astype(jnp.float32).T
    real, imag = by_input[:half], by_input[half:]
    out_ref[:half] = jnp.concatenate([real, imag], axis=1).astype(jnp.bfloat16)
    out_ref[half:] = jnp.concatenate([-imag, real], axis=1).astype(jnp.bfloat16)


def real_form(full):
    orders, half, width = full.shape
    return pl.pallas_call(
        real_form_body,
        grid=(orders,),
        out_shape=jax.ShapeDtypeStruct((orders * width, width), jnp.bfloat16),
        in_specs=[pl.BlockSpec((1, half, width), lambda order: (order, 0, 0))],
        out_specs=pl.BlockSpec((width, width), lambda order: (order, 0)),
        compiler_params=pltpu.CompilerParams(vmem_limit_bytes=24 * 1024 * 1024),
        name="real_form",
    )(full)


def couple_plain(gates, data, weights):
    blocks, lines, width = data.shape
    half = width // 2
    orders = gates.shape[1]
    stations = blocks * BLADES
    norm = 1.0 / math.sqrt(stations)
    results = []
    for low, high, at in windows(lines // BLADES):
        values = data[:, low:high].reshape(blocks * (high - low), width)
        turned = jnp.concatenate([values[:, half:], -values[:, :half]], axis=1)
        spectrum = jnp.dot(
            jnp.asarray(forward_matrix(stations, high - low, at, True)),
            jnp.concatenate([values, values, turned, turned], axis=0),
            preferred_element_type=jnp.float32,
        )
        modes = (spectrum * norm).astype(jnp.bfloat16).reshape(blocks, ROWS, width)
        moved = [
            jnp.roll(modes, orders // 2 - order, axis=0) * gates[:, order].astype(jnp.bfloat16)[:, None, None]
            for order in range(orders)
        ]
        coupled = jnp.dot(
            jnp.concatenate(moved, axis=-1).reshape(blocks * ROWS, orders * width),
            weights,
            preferred_element_type=jnp.float32,
        ).astype(jnp.bfloat16)
        turned = jnp.concatenate([-coupled[:, half:], coupled[:, :half]], axis=1)
        result = jnp.dot(
            jnp.asarray(inverse_matrix(stations, high - low, at)),
            jnp.concatenate([coupled, turned], axis=0),
            preferred_element_type=jnp.float32,
        )
        own = (result * norm).astype(jnp.bfloat16).reshape(blocks, high - low, width)
        results.append(own[:, at : at + BLADES])
    joined = jnp.concatenate(results, axis=1)
    return jnp.pad(joined, ((0, 0), (0, lines - joined.shape[1]), (0, 0)))


def swap(values, axis):
    return lax.ppermute(values, axis, [(0, 1), (1, 0)])


def in_order(first, other, axis):
    mine_first = lax.axis_index(axis) == 0
    return jnp.stack([jnp.where(mine_first, first, other), jnp.where(mine_first, other, first)])


def shards(field, jacobian, coupling):
    local_stations, axial_count, freq_count, width = field.shape
    orders, _, _, own_rows, half = jacobian.shape
    peers = ("freq", "rest")
    rest = lax.axis_size("rest")
    groups = lax.axis_size("group")
    nodes = freq_count * rest
    items = axial_count // rest
    parts = groups * rest

    shared = groups == 2 and rest == 2 and own_rows % 2 == 0
    if shared:
        piece = own_rows // 2
        rows = jacobian.reshape(orders, freq_count, 2, 2, piece, half).transpose(3, 1, 0, 4, 2, 5)
        mine = lax.dynamic_index_in_dim(rows, lax.axis_index("group"), 0, keepdims=False)
        chip = lax.axis_index("freq")
        got = []
        for step in range(freq_count):
            block = lax.dynamic_index_in_dim(mine, chip ^ step, 0, keepdims=False)
            pairs = [(index, index ^ step) for index in range(freq_count)]
            got.append(lax.ppermute(block, "freq", pairs) if step else block)
    else:
        rows = jnp.concatenate([jacobian[:, :, 0], jacobian[:, :, 1]], axis=-1)
        rows = rows.transpose(1, 0, 2, 3).reshape(freq_count, 1, orders * own_rows, width)
        rows = jnp.broadcast_to(rows, (freq_count, rest, orders * own_rows, width))
        got = lax.all_to_all(rows.reshape(nodes, orders * own_rows, width), peers, 0, 0, tiled=True)

    fits = nodes * local_stations <= 704 and items * local_stations % 8 == 0
    if fits:
        packed = pack(field, rest).reshape(nodes, items * local_stations, width)
    else:
        packed = field.reshape(local_stations, rest, items, freq_count, width).transpose(3, 1, 2, 0, 4)
        packed = packed.reshape(nodes, items * local_stations, width)
    lines = round_up(items * local_stations, 8)
    if lines != packed.shape[1]:
        packed = jnp.pad(packed, ((0, 0), (0, lines - packed.shape[1]), (0, 0)))
    got, packed = lax.optimization_barrier((got, packed))
    data = lax.all_to_all(packed, peers, 0, 0, tiled=True)

    if shared:
        ordered = jnp.stack(got)
        for bit in range(freq_count.bit_length() - 1):
            halves = ordered.reshape((freq_count >> (bit + 1), 2, 1 << bit) + ordered.shape[1:])
            flipped = jnp.where((chip >> bit) & 1 == 1, halves[:, ::-1], halves)
            ordered = flipped.reshape(ordered.shape)
        both = in_order(ordered, swap(ordered, "group"), "group")
        full = in_order(both, swap(both, "rest"), "rest")
        full = full.transpose(3, 2, 0, 1, 4, 5, 6)
    else:
        full = got.reshape(nodes, orders, own_rows, width).transpose(1, 0, 2, 3)
    full = full.reshape(orders, nodes * own_rows, width)
    weights = real_form(full)

    result = (couple if fits else couple_plain)(coupling, data, weights)
    returned = lax.all_to_all(result, peers, 0, 0, tiled=True)
    if fits:
        return unpack(returned.reshape(freq_count, rest, items * local_stations, width), axial_count)
    returned = returned[:, : items * local_stations]
    returned = returned.reshape(freq_count, rest, items, local_stations, width).transpose(3, 1, 2, 0, 4)
    return returned.reshape(local_stations, axial_count, freq_count, width)


def solution(mesh):
    names = tuple(mesh.axis_names)
    sizes = dict(mesh.shape)

    def whole(field, jacobian, coupling):
        freq_count = field.shape[2]
        devices = mesh.devices.reshape(sizes[names[0]], freq_count, sizes[names[1]] // freq_count)
        finer = Mesh(devices, ("group", "freq", "rest"))
        every = P(("group", "freq", "rest"), None, None, None)
        placed = (every, P(None, None, None, ("freq", "rest"), None), P())
        return jax.shard_map(shards, mesh=finer, in_specs=placed, out_specs=every, check_vma=False)(
            field, jacobian, coupling
        )

    return whole
```

```python
import functools
import math

import jax
import jax.numpy as jnp
import ml_dtypes
import numpy as np
from jax import lax
from jax.experimental import pallas as pl
from jax.experimental.pallas import tpu as pltpu
from jax.sharding import Mesh
from jax.sharding import PartitionSpec as P

BLADES = 22
ROWS = 24


def round_up(value, multiple):
    return -(-value // multiple) * multiple


def windows(items):
    spans = []
    for item in range(items):
        first = BLADES * item
        low = first // 8 * 8
        spans.append((low, round_up(first + BLADES, 8), first - low))
    return spans


@functools.lru_cache(maxsize=None)
def phases(stations):
    index = np.arange(stations, dtype=np.int64)
    angle = (index[:, None] * index[None, :] % stations) * (2.0 * math.pi / stations)
    blocks = stations // BLADES
    shape = (blocks, BLADES, blocks, BLADES)
    return np.cos(angle).reshape(shape), np.sin(angle).reshape(shape)


def spread(block, row_span, row_at, col_span, col_at):
    count = block.shape[0]
    wide = np.zeros((count, row_span, count, col_span), np.float64)
    wide[:, row_at : row_at + BLADES, :, col_at : col_at + BLADES] = block
    return wide.reshape(count * row_span, count * col_span)


def rounded(values):
    return values.astype(np.float32).astype(ml_dtypes.bfloat16)


@functools.lru_cache(maxsize=None)
def forward_matrix(stations, span, at, split):
    pieces = []
    for part in phases(stations):
        exact = spread(part, ROWS, 0, span, at)
        head = rounded(exact)
        pieces.append(head)
        if split:
            pieces.append(rounded(exact - head.astype(np.float64)))
    return np.concatenate(pieces, axis=1)


@functools.lru_cache(maxsize=None)
def inverse_matrix(stations, span, at):
    return np.concatenate([rounded(spread(part, span, at, ROWS, 0)) for part in phases(stations)], axis=1)


def product(read, right, count, pieces):
    size = count // pieces
    parts = [
        jnp.dot(read(piece * size, size), right, preferred_element_type=jnp.float32) for piece in range(pieces)
    ]
    return jnp.concatenate(parts, axis=0)


def make_kernel(blocks, items, orders, width, split, spans, group):
    half = width // 2
    reach = orders // 2
    lines = round_up(ROWS * group, 16)
    norm = 1.0 / math.sqrt(blocks * BLADES)

    def body(gate_ref, *rest):
        count = 2 + 2 * items
        far, out_hbm, near = rest[:count], rest[count], rest[count + 1 : 2 * count + 1]
        modes_ref, moved_ref, out_ref, sems, out_sems = rest[2 * count + 1 :]
        data_ref, weight_ref = near[0], near[1]
        forward_refs, inverse_refs = near[2 : 2 + items], near[2 + items :]
        copies = [pltpu.make_async_copy(far[index], near[index], sems.at[index]) for index in range(count)]
        order_of_use = [0]
        for start in range(0, items, group):
            order_of_use += [2 + item for item in range(start, start + group)]
            order_of_use += [1] if start == 0 else []
            order_of_use += [2 + items + item for item in range(start, start + group)]
        for index in order_of_use:
            copies[index].start()
        copies[0].wait()
        leaving = []
        tail = None
        tail_at = 0
        for start in range(0, items, group):
            spectra = []
            for item in range(start, start + group):
                low, high, _ = spans[item]
                copies[2 + item].wait()
                values = data_ref[:, low:high, :].reshape(blocks * (high - low), width)
                turned = jnp.concatenate([values[:, half:], -values[:, :half]], axis=1)
                stack = [values, values, turned, turned] if split else [values, turned]
                forward_ref = forward_refs[item]
                spectrum = product(
                    lambda first, size, ref=forward_ref: ref[first : first + size],
                    jnp.concatenate(stack, axis=0),
                    blocks * ROWS,
                    2,
                )
                spectra.append((spectrum * norm).reshape(blocks, ROWS, width))
            if lines > ROWS * group:
                spectra.append(jnp.zeros((blocks, lines - ROWS * group, width), jnp.float32))
            modes = jnp.concatenate(spectra, axis=1).astype(jnp.bfloat16)
            modes_ref[reach : reach + blocks] = modes
            modes_ref[:reach] = modes[blocks - reach :]
            modes_ref[reach + blocks :] = modes[:reach]
            for order in range(orders):
                for block in range(blocks):
                    piece = modes_ref[block + order]
                    keep = gate_ref[block, order] != 0
                    moved_ref[block, :, order * width : (order + 1) * width] = jnp.where(
                        keep, piece, jnp.zeros_like(piece)
                    )
            if start == 0:
                copies[1].wait()
            coupled = product(
                lambda first, size: moved_ref[first : first + size].reshape(size * lines, orders * width),
                weight_ref[...],
                blocks,
                2,
            ).reshape(blocks, lines, width)
            for offset in range(group):
                item = start + offset
                low, high, _ = spans[item]
                own = coupled[:, offset * ROWS : (offset + 1) * ROWS].reshape(blocks * ROWS, width)
                own = own.astype(jnp.bfloat16)
                copies[2 + items + item].wait()
                turned = jnp.concatenate([-own[:, half:], own[:, :half]], axis=1)
                inverse_ref = inverse_refs[item]
                result = product(
                    lambda first, size, ref=inverse_ref: ref[first : first + size],
                    jnp.concatenate([own, turned], axis=0),
                    blocks * (high - low),
                    2,
                ).reshape(blocks, high - low, width)
                if tail is not None and tail_at == low:
                    joined = result[:, :8] + tail
                    result = jnp.concatenate([joined, result[:, 8:]], axis=1)
                last = item == items - 1 or spans[item + 1][0] >= high
                stop = high if last else spans[item + 1][0]
                out_ref[:, low:stop, :] = (result[:, : stop - low] * norm).astype(jnp.bfloat16)
                leaving.append(
                    pltpu.make_async_copy(out_ref.at[:, low:stop], out_hbm.at[:, low:stop], out_sems.at[item])
                )
                leaving[-1].start()
                tail = None if last else result[:, stop - low :]
                tail_at = stop
        for copy in leaving:
            copy.wait()

    return body


def couple(gates, data, weights):
    blocks, lines, width = data.shape
    items = lines // BLADES
    orders = gates.shape[1]
    stations = blocks * BLADES
    spans = windows(items)
    group = 2 if items % 2 == 0 else 1
    split = True
    forward = [jnp.asarray(forward_matrix(stations, high - low, at, split)) for low, high, at in spans]
    inverse = [jnp.asarray(inverse_matrix(stations, high - low, at)) for low, high, at in spans]
    rows = round_up(ROWS * group, 16)
    operands = [data, weights, *forward, *inverse]
    return pl.pallas_call(
        make_kernel(blocks, items, orders, width, split, spans, group),
        out_shape=jax.ShapeDtypeStruct(data.shape, jnp.bfloat16),
        in_specs=[pl.BlockSpec(memory_space=pltpu.SMEM)] + [pl.BlockSpec(memory_space=pltpu.HBM)] * len(operands),
        out_specs=pl.BlockSpec(memory_space=pltpu.HBM),
        scratch_shapes=[pltpu.VMEM(operand.shape, operand.dtype) for operand in operands]
        + [
            pltpu.VMEM((blocks + orders - 1, rows, width), jnp.bfloat16),
            pltpu.VMEM((blocks, rows, orders * width), jnp.bfloat16),
            pltpu.VMEM(data.shape, jnp.bfloat16),
            pltpu.SemaphoreType.DMA((len(operands),)),
            pltpu.SemaphoreType.DMA((items,)),
        ],
        compiler_params=pltpu.CompilerParams(vmem_limit_bytes=60 * 1024 * 1024),
        name="couple",
    )(gates, *operands)


@functools.lru_cache(maxsize=None)
def reorder_matrix(stations, items, freqs):
    rows = np.arange(stations * items * freqs).reshape(stations, items, freqs).transpose(2, 1, 0).reshape(-1)
    return (rows[:, None] == np.arange(rows.size)[None, :]).astype(ml_dtypes.bfloat16)


def reorder_body(matrix_ref, in_ref, out_ref):
    width = in_ref.shape[-1]
    moved = product(
        lambda first, size: matrix_ref[first : first + size], in_ref[...].reshape(-1, width), matrix_ref.shape[0], 2
    )
    out_ref[...] = moved.astype(jnp.bfloat16).reshape(out_ref.shape)


def pack(field, rest):
    stations, axials, freqs, width = field.shape
    items = axials // rest
    matrix = jnp.asarray(reorder_matrix(stations, items, freqs))
    return pl.pallas_call(
        reorder_body,
        grid=(rest,),
        out_shape=jax.ShapeDtypeStruct((freqs, rest, items * stations, width), jnp.bfloat16),
        in_specs=[
            pl.BlockSpec(matrix.shape, lambda part: (0, 0)),
            pl.BlockSpec((stations, items, freqs, width), lambda part: (0, part, 0, 0)),
        ],
        out_specs=pl.BlockSpec((freqs, 1, items * stations, width), lambda part: (0, part, 0, 0)),
        compiler_params=pltpu.CompilerParams(vmem_limit_bytes=32 * 1024 * 1024),
        name="pack",
    )(matrix, field)


def unpack(values, axials):
    freqs, rest, lines, width = values.shape
    items = axials // rest
    stations = lines // items
    matrix = jnp.asarray(reorder_matrix(stations, items, freqs).T)
    return pl.pallas_call(
        reorder_body,
        grid=(rest,),
        out_shape=jax.ShapeDtypeStruct((stations, axials, freqs, width), jnp.bfloat16),
        in_specs=[
            pl.BlockSpec(matrix.shape, lambda part: (0, 0)),
            pl.BlockSpec((freqs, 1, lines, width), lambda part: (0, part, 0, 0)),
        ],
        out_specs=pl.BlockSpec((stations, items, freqs, width), lambda part: (0, part, 0, 0)),
        compiler_params=pltpu.CompilerParams(vmem_limit_bytes=32 * 1024 * 1024),
        name="unpack",
    )(matrix, values)


def real_form_body(in_ref, out_ref):
    width = in_ref.shape[-1]
    half = width // 2
    by_input = in_ref[0].astype(jnp.float32).T
    real, imag = by_input[:half], by_input[half:]
    out_ref[:half] = jnp.concatenate([real, imag], axis=1).astype(jnp.bfloat16)
    out_ref[half:] = jnp.concatenate([-imag, real], axis=1).astype(jnp.bfloat16)


def real_form(full):
    orders, half, width = full.shape
    return pl.pallas_call(
        real_form_body,
        grid=(orders,),
        out_shape=jax.ShapeDtypeStruct((orders * width, width), jnp.bfloat16),
        in_specs=[pl.BlockSpec((1, half, width), lambda order: (order, 0, 0))],
        out_specs=pl.BlockSpec((width, width), lambda order: (order, 0)),
        compiler_params=pltpu.CompilerParams(vmem_limit_bytes=24 * 1024 * 1024),
        name="real_form",
    )(full)


def couple_plain(gates, data, weights):
    blocks, lines, width = data.shape
    half = width // 2
    orders = gates.shape[1]
    stations = blocks * BLADES
    norm = 1.0 / math.sqrt(stations)
    results = []
    for low, high, at in windows(lines // BLADES):
        values = data[:, low:high].reshape(blocks * (high - low), width)
        turned = jnp.concatenate([values[:, half:], -values[:, :half]], axis=1)
        spectrum = jnp.dot(
            jnp.asarray(forward_matrix(stations, high - low, at, True)),
            jnp.concatenate([values, values, turned, turned], axis=0),
            preferred_element_type=jnp.float32,
        )
        modes = (spectrum * norm).astype(jnp.bfloat16).reshape(blocks, ROWS, width)
        moved = [
            jnp.roll(modes, orders // 2 - order, axis=0) * gates[:, order].astype(jnp.bfloat16)[:, None, None]
            for order in range(orders)
        ]
        coupled = jnp.dot(
            jnp.concatenate(moved, axis=-1).reshape(blocks * ROWS, orders * width),
            weights,
            preferred_element_type=jnp.float32,
        ).astype(jnp.bfloat16)
        turned = jnp.concatenate([-coupled[:, half:], coupled[:, :half]], axis=1)
        result = jnp.dot(
            jnp.asarray(inverse_matrix(stations, high - low, at)),
            jnp.concatenate([coupled, turned], axis=0),
            preferred_element_type=jnp.float32,
        )
        own = (result * norm).astype(jnp.bfloat16).reshape(blocks, high - low, width)
        results.append(own[:, at : at + BLADES])
    joined = jnp.concatenate(results, axis=1)
    return jnp.pad(joined, ((0, 0), (0, lines - joined.shape[1]), (0, 0)))


def swap(values, axis):
    return lax.ppermute(values, axis, [(0, 1), (1, 0)])


def in_order(first, other, axis):
    mine_first = lax.axis_index(axis) == 0
    return jnp.stack([jnp.where(mine_first, first, other), jnp.where(mine_first, other, first)])


def shards(field, jacobian, coupling):
    local_stations, axial_count, freq_count, width = field.shape
    orders, _, _, own_rows, half = jacobian.shape
    peers = ("freq", "rest")
    rest = lax.axis_size("rest")
    groups = lax.axis_size("group")
    nodes = freq_count * rest
    items = axial_count // rest
    parts = groups * rest

    shared = groups == 2 and rest == 2 and own_rows % 2 == 0
    if shared:
        piece = own_rows // 2
        rows = jacobian.reshape(orders, freq_count, 2, 2, piece, half).transpose(3, 1, 0, 4, 2, 5)
        mine = lax.dynamic_index_in_dim(rows, lax.axis_index("group"), 0, keepdims=False)
        chip = lax.axis_index("freq")
        got = []
        for step in range(freq_count):
            block = lax.dynamic_index_in_dim(mine, chip ^ step, 0, keepdims=False)
            pairs = [(index, index ^ step) for index in range(freq_count)]
            got.append(lax.ppermute(block, "freq", pairs) if step else block)
    else:
        rows = jnp.concatenate([jacobian[:, :, 0], jacobian[:, :, 1]], axis=-1)
        rows = rows.transpose(1, 0, 2, 3).reshape(freq_count, 1, orders * own_rows, width)
        rows = jnp.broadcast_to(rows, (freq_count, rest, orders * own_rows, width))
        got = lax.all_to_all(rows.reshape(nodes, orders * own_rows, width), peers, 0, 0, tiled=True)

    fits = nodes * local_stations <= 704 and items * local_stations % 8 == 0
    if fits:
        packed = pack(field, rest).reshape(nodes, items * local_stations, width)
    else:
        packed = field.reshape(local_stations, rest, items, freq_count, width).transpose(3, 1, 2, 0, 4)
        packed = packed.reshape(nodes, items * local_stations, width)
    lines = round_up(items * local_stations, 8)
    if lines != packed.shape[1]:
        packed = jnp.pad(packed, ((0, 0), (0, lines - packed.shape[1]), (0, 0)))
    got, packed = lax.optimization_barrier((got, packed))
    data = lax.all_to_all(packed, peers, 0, 0, tiled=True)

    if shared:
        ordered = jnp.stack(got)
        for bit in range(freq_count.bit_length() - 1):
            halves = ordered.reshape((freq_count >> (bit + 1), 2, 1 << bit) + ordered.shape[1:])
            flipped = jnp.where((chip >> bit) & 1 == 1, halves[:, ::-1], halves)
            ordered = flipped.reshape(ordered.shape)
        both = in_order(ordered, swap(ordered, "group"), "group")
        full = in_order(both, swap(both, "rest"), "rest")
        full = full.transpose(3, 2, 0, 1, 4, 5, 6)
    else:
        full = got.reshape(nodes, orders, own_rows, width).transpose(1, 0, 2, 3)
    full = full.reshape(orders, nodes * own_rows, width)
    weights = real_form(full)

    result = (couple if fits else couple_plain)(coupling, data, weights)
    returned = lax.all_to_all(result, peers, 0, 0, tiled=True)
    if fits:
        return unpack(returned.reshape(freq_count, rest, items * local_stations, width), axial_count)
    returned = returned[:, : items * local_stations]
    returned = returned.reshape(freq_count, rest, items, local_stations, width).transpose(3, 1, 2, 0, 4)
    return returned.reshape(local_stations, axial_count, freq_count, width)


def solution(mesh):
    names = tuple(mesh.axis_names)
    sizes = dict(mesh.shape)

    def whole(field, jacobian, coupling):
        freq_count = field.shape[2]
        devices = mesh.devices.reshape(sizes[names[0]], freq_count, sizes[names[1]] // freq_count)
        finer = Mesh(devices, ("group", "freq", "rest"))
        every = P(("group", "freq", "rest"), None, None, None)
        placed = (every, P(None, None, None, ("freq", "rest"), None), P())
        return jax.shard_map(shards, mesh=finer, in_specs=placed, out_specs=every, check_vma=False)(
            field, jacobian, coupling
        )

    return whole
```
